32 devices in a mesh: dp: 8 (over z, core), fsdp: 4 (over y, x).
Axes of the slice: x: 2, y: 2, z: 4, core: 2. Of those that a mesh axis runs over, the one named last changes fastest.
Arguments:
- old_weight: float32 [8192, 1024], P('dp', 'fsdp'), may hold values from -6 to 6
- old_first: float32 [8192, 1024], P('dp', 'fsdp'), may hold values from -6 to 6
- old_second: float32 [8192, 1024], P('dp', 'fsdp'), may hold values from 0.01 to 1
- grads: bfloat16 [8, 8, 1024, 1024], P('dp', None, 'fsdp'), may hold values from -60 to 60
- column_shard_lookup: int32 [8, 4], P('dp'), may hold values from 0 to 3, each once within a row
- alive: int32 [8], replicated, may hold values from 0 to 1, as said below
Outputs:
- new_weight: float32 [8192, 1024], P(('dp', 'fsdp'))
- new_first: float32 [8192, 1024], P(('dp', 'fsdp'))
- second_moment_next: float32 [8192, 1024], P(('dp', 'fsdp'))
The draws below stay inside these ranges and needn't reach their ends.
Inputs may be any that keep to these rules, and one draw needn't show every extreme that they name: `column_shard_lookup`: each row is a permutation of 0 to 3. `alive`: at least 4 entries are 1 and at least one is 0.
All inputs are finite; a program needn't handle non-finite values.
Results may differ from the reference program's by a relative error of at most 0.0003.
Values sent between devices are 32-bit elements; how exact they have to be, the bound alone decides.
A program may use at most 64 MiB of HBM per device.

```python
import math
import jax
import jax.numpy as jnp
from jax import lax

D = 8192
KV = 1024
STEP = 1000
DP = 8
OLD_ROWS = 1024
N_DP = 8
N_FSDP = 4


def draw_alive(key, part):
    first_key, second_key = jax.random.split(jax.random.fold_in(key, 11))
    live_count = jax.random.randint(first_key, (), DP // 2, DP)
    ranking = jax.random.permutation(second_key, DP)
    return (ranking < live_count).astype(jnp.int32)


def raised(entries, own_key, source, target, parts, factor):
    owner, partner = [(jnp.arange(entries.shape[axis_at]) // (entries.shape[axis_at] // parts)).reshape([-1 if axis == axis_at else 1 for axis in range(entries.ndim)]) for axis_at in (source, target)]
    chosen = jax.random.permutation(own_key, parts)[partner]
    strong = (owner == chosen) | (owner == (partner + parts // 2) % parts)
    return jnp.where(strong, factor * entries, entries)


def shard_levels(own_key, extent, cuts, least, high):
    factor_of = 1.0
    for dim, blocks in cuts:
        heights = jax.random.uniform(jax.random.fold_in(jax.random.fold_in(own_key, 6), dim), (blocks,), jnp.float32, least / len(cuts), high / len(cuts))
        factor_of = factor_of * jnp.repeat(jnp.exp(heights), extent[dim] // blocks).reshape((-1,) + (1,) * (len(extent) - 1 - dim))
    return factor_of


def normal_values(key, shape, deviation, limit, cuts=(), held_as=jnp.bfloat16):
    array = deviation * jax.random.normal(key, shape, jnp.float32)
    if cuts:
        array = array * shard_levels(key, shape, cuts, -0.22, 0.18)
    return jnp.clip(array, -limit, limit).astype(held_as)


def noise_with(own_key, shape, width, bound, cuts, heavy, dtype=jnp.bfloat16):
    array = width * jax.random.normal(own_key, shape, jnp.float32)
    if cuts:
        array = array * shard_levels(own_key, shape, cuts, -0.22, 0.18)
    return jnp.clip(raised(array, jax.random.fold_in(own_key, 3), *heavy), -bound, bound).astype(dtype)


def setup_inputs(seed: int = 0) -> dict:
    streams_of = jax.random.split(jax.random.key(seed), 7)
    old_weight = normal_values(streams_of[0], (D, KV), 1.0, 6.0, ((0, 8), (1, 4)), jnp.float32)
    old_first = normal_values(streams_of[1], (D, KV), 1.0, 6.0, ((0, 8), (1, 4)), jnp.float32)
    old_second = jnp.clip(jnp.exp(math.log(1.0) - 4.6051702 * jax.random.uniform(streams_of[2], (D, KV), jnp.float32) ** shard_levels(streams_of[2], (D, KV), ((0, 8), (1, 4)), -0.2, 0.2)), 0.01, 1.0)
    grads = noise_with(streams_of[3], (DP, DP, OLD_ROWS, KV), 10.0, 60.0, ((0, 8), (2, 4)), (0, 1, 8, 2.0))
    column_shard_lookup = jax.vmap(lambda own: jax.random.permutation(own, N_FSDP))(jax.random.split(streams_of[4], DP)).reshape((DP, N_FSDP)).astype(jnp.int32)
    alive = draw_alive(jax.random.fold_in(streams_of[6], 71), 0)
    return {"old_weight": old_weight, "old_first": old_first, "old_second": old_second, "grads": grads, "column_shard_lookup": column_shard_lookup, "alive": alive}


def restore(saved, column_order):
    blocks = saved.reshape(N_DP, D // N_DP, N_FSDP, KV // N_FSDP)
    placed = jnp.take_along_axis(blocks, column_order[:, None, :, None], axis=2)
    return placed.reshape(D, KV)

def apply_adamw(weight, first, second, gradient_matrix):
    first_new = 0.9 * first + 0.1 * gradient_matrix
    second_new = 0.95 * second + 0.05 * gradient_matrix * gradient_matrix
    first_hat = first_new / (1.0 - 0.9 ** STEP)
    second_corrected = second_new / (1.0 - 0.95 ** STEP)
    weight_new = weight - 0.02 * (first_hat / (jnp.sqrt(second_corrected) + 1e-08) + 0.25 * weight)
    return (weight_new, first_new, second_new)

def reference(old_weight, old_first, old_second, grads, column_shard_lookup, alive):
    column_order = jnp.argsort(column_shard_lookup, axis=1).astype(jnp.int32)
    weight = restore(old_weight, column_order)
    first = restore(old_first, column_order)
    second = restore(old_second, column_order)
    live_mask = alive.astype(jnp.float32)

    def accumulate(running, inputs):
        partial_grad, weight_live = inputs
        return (running + partial_grad.astype(jnp.float32) * weight_live, None)
    start = jnp.zeros((N_DP, D // N_DP, KV), jnp.float32)
    reduced_total, unused = lax.scan(accumulate, start, (grads, live_mask))
    gradient_matrix = reduced_total.reshape(D, KV) / jnp.sum(live_mask)
    return apply_adamw(weight, first, second, gradient_matrix)
```

```python
import jax
import jax.numpy as jnp
from jax import lax
from jax.sharding import PartitionSpec as P

STEP = 1000


def restore_columns(block, lookup, shards):
    rows = block.shape[0] // shards
    pieces = [block[held * rows : (held + 1) * rows] for held in range(shards)]
    columns = []
    for place in range(shards):
        chosen = pieces[0]
        for held in range(1, shards):
            chosen = jnp.where(lookup[held] == place, pieces[held], chosen)
        columns.append(chosen)
    return jnp.concatenate(columns, axis=1)


def body(old_weight, old_first, old_second, grads, column_shard_lookup, alive):
    shards = lax.axis_size("fsdp")
    live_mask = alive.astype(jnp.float32)
    remaining_entries = jnp.sum(live_mask)
    own_live = lax.dynamic_index_in_dim(live_mask, lax.axis_index("dp"), 0, keepdims=False)
    partial_grad = grads[0].reshape(-1, grads.shape[3])
    masked = partial_grad.astype(jnp.float32) * own_live
    reduced_total = lax.psum_scatter(masked, "dp", scatter_dimension=0, tiled=True)
    lookup = column_shard_lookup[0]
    weight, first, second = [
        restore_columns(lax.all_to_all(state, "fsdp", split_axis=0, concat_axis=0, tiled=True), lookup, shards)
        for state in (old_weight, old_first, old_second)
    ]
    gradient_matrix = reduced_total / remaining_entries
    first_new = 0.9 * first + 0.1 * gradient_matrix
    second_new = 0.95 * second + 0.05 * gradient_matrix * gradient_matrix
    first_hat = first_new / (1.0 - 0.9**STEP)
    second_corrected = second_new / (1.0 - 0.95**STEP)
    weight_new = weight - 0.02 * (first_hat / (jnp.sqrt(second_corrected) + 1e-08) + 0.25 * weight)
    return (weight_new, first_new, second_new)


def solution(mesh):
    return jax.shard_map(
        body,
        mesh=mesh,
        in_specs=(
            P("dp", "fsdp"),
            P("dp", "fsdp"),
            P("dp", "fsdp"),
            P("dp", None, "fsdp", None),
            P("dp", None),
            P(),
        ),
        out_specs=(P(("dp", "fsdp"), None), P(("dp", "fsdp"), None), P(("dp", "fsdp"), None)),
        check_vma=False,
    )
```
